32 devices in a mesh: groups: 2 (over y), tile: 4 (over z), plane: 2 (over x), inst: 2 (over core).
Axes of the slice: x: 2, y: 2, z: 4, core: 2. Of those that a mesh axis runs over, the one named last changes fastest.
Arguments:
- state: float32 [48, 10, 2, 32, 128], P('inst', 'groups', 'plane', 'tile'), parts along dimension 1, may hold values from -6 to 6
- boundary: float32 [48, 2, 10, 32, 128], P('inst', None, 'groups', ('tile', 'plane')), parts along dimension 2, may hold values from -6 to 6
- inv_volume: float32 [4, 32, 128], P(('groups', 'plane'), 'tile'), parts along dimension 0, may hold values from 0.5 to 2
- flux_matrix: float32 [6, 5, 5], P('groups'), parts along dimension 0, may hold values from -2.5 to 2.5
- left_vectors: float32 [10, 5], P('groups'), parts along dimension 0, may hold values from -2.5 to 2.5
- right_vectors: float32 [10, 5], P('groups'), parts along dimension 0, may hold values from -2.5 to 2.5
- gain: float32 [4, 2, 64, 2, 3], P('groups'), parts along dimension 0, may hold values from -3 to 3
- harmonic_index: int32 [40], P('groups'), parts along dimension 0, may hold values from 1 to 23, as said below
- mode_count: int32 [4, 128], P('groups'), parts along dimension 0, may hold values from 1 to 64
Outputs:
- residual: float32 [48, 10, 2, 32, 128], P('inst', 'groups', 'plane', 'tile'), parts along dimension 1
- corrected: float32 [48, 2, 10, 32, 128], P('inst', None, 'groups', ('tile', 'plane')), parts along dimension 2
The draws below stay inside these ranges and needn't reach their ends.
There are 2 independent parts, one for each index of `groups`. The reference program is written for one: setup_inputs(seed, part) draws one part's arguments, and reference() takes and returns one part's arrays. A program takes and returns all parts, laid end to end along the dimension named above; each array names one. Nothing has to cross between parts.
Inputs may be any that keep to these rules, and one draw needn't show every extreme that they name: `harmonic_index`: 20 distinct values in rising order; the first is 1 and the last is 23.
All inputs are finite; a program needn't handle non-finite values.
Results may differ from the reference program's by a relative error of at most 0.0001.
Values sent between devices are 32-bit elements; how exact they have to be, the bound alone decides.
No kernel may reach another device: no remote copies, remote signals or barrier semaphores. Data moves between devices by JAX's collectives and lax.ppermute only.
A program may use at most 64 MiB of HBM per device.

```python
import math
import jax
import jax.numpy as jnp
from jax import lax

NV = 5
NI = 2
NO = 3
NT = 48
KH = 20
MODES = 64
NR = 128
NC = 32
NA = 2


def draw_harmonic_index(key, part):
    middle = jax.random.permutation(jax.random.fold_in(key, 11), NT // 2 - 3).astype(jnp.int32) + 2
    chosen = middle[:KH - 2]
    ends = jnp.array([1, NT // 2 - 1], dtype=jnp.int32)
    return jnp.sort(jnp.concatenate([ends, chosen]))


def with_ends(values, rng, low, top_value):
    dims = values.shape
    place = [jax.random.randint(jax.random.fold_in(rng, axis), (), 0, dims[axis]) for axis in range(len(dims))]
    values = values.at[tuple(place)].set(low)
    longest = dims.index(max(dims))
    place[longest] = (place[longest] + 1) % dims[longest]
    return values.at[tuple(place)].set(top_value)


def level_of(rng, dims, split, smallest, largest):
    level, own = 1.0, jax.random.fold_in(rng, 6)
    for dim, parts in split:
        heights = jnp.exp(jax.random.uniform(jax.random.fold_in(own, dim), (parts,), jnp.float32, smallest / len(split), largest / len(split)))
        level = level * jnp.repeat(heights, dims[dim] // parts).reshape([-1 if axis == dim else 1 for axis in range(len(dims))])
    return level


def scatter_about(rng, shape, spread, limit, cuts=(), kind=jnp.bfloat16):
    entries = spread * jax.random.normal(rng, shape, jnp.float32)
    if cuts:
        entries = entries * level_of(rng, shape, cuts, -0.22, 0.18)
    return jnp.clip(entries, -limit, limit).astype(kind)


def setup_inputs(seed: int = 0, part: int = 0) -> dict:
    arg_keys = jax.random.split(jax.random.key(seed), 10)
    part_splits = jax.random.split(jax.random.fold_in(arg_keys[9], part), 10)
    return {
        "state": scatter_about(part_splits[0], (NT, NV, NA, NC, NR), 1.0, 6.0, ((0, 2), (2, 2), (3, 4)), jnp.float32),
        "boundary": scatter_about(part_splits[1], (NT, 2, NV, NC, NR), 1.0, 6.0, ((0, 2), (3, 8)), jnp.float32),
        "inv_volume": jnp.clip(jnp.exp(math.log(2.0) - 1.3862944 * jax.random.uniform(part_splits[2], (NA, NC, NR), jnp.float32) ** level_of(part_splits[2], (NA, NC, NR), ((0, 2), (1, 4)), -0.2, 0.2)), 0.5, 2.0),
        "flux_matrix": scatter_about(part_splits[3], (3, NV, NV), NV ** -0.5, 2.5, (), jnp.float32),
        "left_vectors": scatter_about(part_splits[4], (NV, NV), NV ** -0.5, 2.5, (), jnp.float32),
        "right_vectors": scatter_about(part_splits[5], (NV, NV), NV ** -0.5, 2.5, (), jnp.float32),
        "gain": scatter_about(part_splits[6], (2, 2, MODES, NI, NO), 0.5, 3.0, (), jnp.float32),
        "harmonic_index": draw_harmonic_index(jax.random.fold_in(jax.random.fold_in(arg_keys[9], part), 71), part),
        "mode_count": with_ends(jax.random.randint(part_splits[8], (2, NR), 1, MODES + 1), jax.random.fold_in(part_splits[8], 1), 1, MODES).astype(jnp.int32),
    }


precise = lax.Precision.HIGHEST
DISSIPATION = 0.25
OMEGA_SCALE = 0.1


def cell_tables(cell_ids, mode_total, period):
    product = (cell_ids[:, None] * jnp.arange(mode_total, dtype=jnp.int32)[None, :]) % period
    phases = product.astype(jnp.float32) * (2.0 * math.pi / period)
    return jnp.cos(phases), jnp.sin(phases)


def time_tables(harmonic_index, instance_ids, period):
    product = (instance_ids[:, None] * harmonic_index[None, :]) % period
    phases = product.astype(jnp.float32) * (2.0 * math.pi / period)
    cos_table = jnp.cos(phases)
    sin_table = jnp.sin(phases)
    frequency = harmonic_index.astype(jnp.float32)[None, :]
    analysis = jnp.concatenate([cos_table, sin_table], axis=1).T * (2.0 / period)
    synthesis = jnp.concatenate([-frequency * sin_table, frequency * cos_table], axis=1) * OMEGA_SCALE
    return analysis, synthesis


def giles_planes(boundary, left_vectors, right_vectors, gain, mode_count):
    cos_table, sin_table = cell_tables(jnp.arange(NC, dtype=jnp.int32), MODES, NC)
    weight = 2.0 / NC
    hat_cos = jnp.einsum("tpvcr,cm->tpvmr", boundary, cos_table * weight, precision=precise)
    hat_sin = jnp.einsum("tpvcr,cm->tpvmr", boundary, sin_table * weight, precision=precise)
    wave_cos = jnp.einsum("uv,tpvmr->tpumr", left_vectors, hat_cos, precision=precise)
    wave_sin = jnp.einsum("uv,tpvmr->tpumr", left_vectors, hat_sin, precision=precise)
    gain_real = gain[:, 0]
    gain_imag = gain[:, 1]
    out_cos = wave_cos[:, :, NI:]
    out_sin = wave_sin[:, :, NI:]
    target_cos = jnp.einsum("pmio,tpomr->tpimr", gain_real, out_cos, precision=precise) - jnp.einsum("pmio,tpomr->tpimr", gain_imag, out_sin, precision=precise)
    target_sin = jnp.einsum("pmio,tpomr->tpimr", gain_imag, out_cos, precision=precise) + jnp.einsum("pmio,tpomr->tpimr", gain_real, out_sin, precision=precise)
    resolved = (jnp.arange(MODES, dtype=jnp.int32)[None, :, None] < mode_count[:, None, :]).astype(jnp.float32)
    jump_cos = (target_cos - wave_cos[:, :, :NI]) * resolved[None, :, None]
    jump_sin = (target_sin - wave_sin[:, :, :NI]) * resolved[None, :, None]
    back_cos = jnp.einsum("ui,tpimr->tpumr", right_vectors[:, :NI], jump_cos, precision=precise)
    back_sin = jnp.einsum("ui,tpimr->tpumr", right_vectors[:, :NI], jump_sin, precision=precise)
    delta = jnp.einsum("tpumr,cm->tpucr", back_cos, cos_table, precision=precise) + jnp.einsum("tpumr,cm->tpucr", back_sin, sin_table, precision=precise)
    return boundary + delta


def reference(state, boundary, inv_volume, flux_matrix, left_vectors, right_vectors, gain, harmonic_index, mode_count):
    corrected = giles_planes(boundary, left_vectors, right_vectors, gain, mode_count)

    def flux_one(inputs):
        field, inlet_layer, exit_layer = inputs
        axial = jnp.concatenate([inlet_layer[:, None], field, exit_layer[:, None]], axis=1)
        radial = jnp.pad(field, ((0, 0), (0, 0), (0, 0), (1, 1)))
        neighbours = ((axial[:, 2:], axial[:, :-2]), (jnp.roll(field, -1, axis=2), jnp.roll(field, 1, axis=2)), (radial[..., 2:], radial[..., :-2]))
        total = jnp.zeros_like(field)
        for direction in range(3):
            forward, backward = neighbours[direction]
            total = total + jnp.einsum("vw,wacr->vacr", flux_matrix[direction], 0.5 * (forward - backward), precision=precise)
            total = total - DISSIPATION * (forward - 2.0 * field + backward)
        return inv_volume[None] * total

    flux = lax.map(flux_one, (state, corrected[:, 0], corrected[:, 1]))
    analysis, synthesis = time_tables(harmonic_index, jnp.arange(NT, dtype=jnp.int32), NT)
    flat_state = state.reshape(NT, -1)
    coefficients = jnp.dot(analysis, flat_state, precision=precise)
    rate = jnp.dot(synthesis, coefficients, precision=precise).reshape(state.shape)
    return flux + rate, corrected
```

```python
import math

import jax
import jax.numpy as jnp
import numpy as np
from jax import lax
from jax.experimental import pallas as pl
from jax.experimental.pallas import tpu as pltpu
from jax.sharding import PartitionSpec as P

NI = 2
DISSIPATION = 0.25
OMEGA_SCALE = 0.1
precise = lax.Precision.HIGHEST
VMEM_SPEC = pl.BlockSpec(memory_space=pltpu.VMEM)
SMEM_SPEC = pl.BlockSpec(memory_space=pltpu.SMEM)


def partner(position, step, count):
    if count == 4:
        return position ^ step, position ^ step
    return (position + step) % count, (position - step) % count


def tile_pairs(step, count):
    return [(i, partner(i, step, count)[0]) for i in range(count)]


def mode_classes(mode_total, period):
    residue = np.arange(mode_total) % period
    classes = np.minimum(residue, period - residue)
    signs = np.where(residue <= period - residue, 1.0, -1.0)
    return classes, signs, min(mode_total, period // 2 + 1)


def fold_tables(mode_total, period):
    classes, signs, count = mode_classes(mode_total, period)
    rows = -(-count // 8) * 8
    fold = np.zeros((rows, mode_total), np.float32)
    fold[classes, np.arange(mode_total)] = 1.0
    return fold, fold * signs.astype(np.float32)[None, :], rows, count


def class_waves(cells, rows, count, period):
    out = np.zeros((2 * rows, len(cells)))
    phase = 2.0 * np.pi * ((np.arange(count)[:, None] * np.asarray(cells)[None, :]) % period) / period
    out[:count] = np.cos(phase)
    out[rows : rows + count] = np.sin(phase)
    return out


def cell_layouts(tiles, planes, face_cells, rows, count):
    cells, period = planes * face_cells, tiles * planes * face_cells
    positions = tiles if tiles == 4 else 1
    forward = np.zeros((positions * planes, 2 * rows, period), np.float32)
    backward = np.zeros((positions * planes, period, 2 * rows), np.float32)
    for position in range(positions):
        for plane in range(planes):
            arrive, depart = [], []
            for step in range(tiles):
                target, source = partner(position, step, tiles)
                for shift in range(planes):
                    other = face_plane(plane, shift, planes)
                    arrive += [source * cells + other * face_cells + k for k in range(face_cells)]
                depart += [target * cells + k for k in range(cells)]
            forward[position * planes + plane] = class_waves(arrive, rows, count, period) * (2.0 / period)
            backward[position * planes + plane] = class_waves(depart, rows, count, period).T
    return forward, backward


def face_plane(plane, shift, planes):
    if shift == 0:
        return plane
    return shift if plane == 0 else planes - 1 - shift


def base_kernel(
    mats, harmonics, state, *rest, inst_count
):
    others = rest[: inst_count - 1]
    inv_volume, sine, gain, station_modes, fold, fold_sine, out, tables, weights = rest[inst_count - 1 :]
    local_count, variables, cells, stations = state.shape
    total = local_count * inst_count
    lane = lax.broadcasted_iota(jnp.int32, (1, sine.shape[1]), 1)
    present = jnp.zeros((1, sine.shape[1]), jnp.float32)
    for k in range(harmonics.shape[0]):
        h = harmonics[k]
        present = present + jnp.where(lane == lax.rem(h, total), h.astype(jnp.float32), 0.0)
    column = jnp.sum(sine[...] * present, axis=1, keepdims=True)
    weights[...] = jnp.broadcast_to(column, weights.shape)

    def rate_of(v, carry):
        sums = [jnp.zeros((cells, stations), jnp.float32) for _ in range(local_count)]
        for block, source in enumerate((state,) + tuple(others)):
            for j in range(local_count):
                value = source[j, v]
                for t in range(local_count):
                    d = (j + block * local_count - t) % total
                    if d:
                        w = jnp.broadcast_to(weights[d : d + 1, :], (cells, stations))
                        sums[t] = sums[t] + w * value
        for t in range(local_count):
            out[t, v] = sums[t]
        return carry

    lax.fori_loop(0, variables, rate_of, 0)
    lanes = lax.broadcasted_iota(jnp.int32, (cells, stations), 1)
    volume = inv_volume[...]

    def radial_of(t, carry):
        half, total_of = [], []
        for w in range(variables):
            s = state[t, w]
            forward = jnp.where(lanes == stations - 1, 0.0, pltpu.roll(s, stations - 1, 1))
            backward = jnp.where(lanes == 0, 0.0, pltpu.roll(s, 1, 1))
            half.append(0.5 * (forward - backward))
            total_of.append((6.0 * DISSIPATION) * s - DISSIPATION * (forward + backward))
        for v in range(variables):
            acc = total_of[v]
            for w in range(variables):
                acc = acc + mats[(2 * variables + v) * variables + w] * half[w]
            out[t, v] = out[t, v] + volume * acc
        return carry

    lax.fori_loop(0, local_count, radial_of, 0)
    modes = fold.shape[1]
    mode = lax.broadcasted_iota(jnp.int32, (modes, station_modes.shape[1]), 0)
    resolved = (mode < station_modes[...]).astype(jnp.float32)
    rows = fold.shape[0]
    parts = [fold[...] * gain[k : k + 1, :] for k in range(6)]
    parts += [fold_sine[...] * gain[k : k + 1, :] for k in range(6, 12)]
    parts.append(fold[...])
    summed = jnp.dot(jnp.concatenate(parts, axis=0), resolved, precision=precise, preferred_element_type=jnp.float32)
    for k in range(13):
        tables[k] = summed[k * rows : (k + 1) * rows]


def jump_kernel(mats, forward, backward, tables, *rest, tiles, planes, offset):
    blocks = rest[: tiles * planes]
    outs = rest[tiles * planes : tiles * planes + tiles]
    gathered = rest[-1]
    count, variables, width, stations = blocks[0].shape
    rows = tables.shape[1]
    cells = outs[0].shape[2]
    count = outs[0].shape[0]
    for b, block in enumerate(blocks):
        for t in range(count):
            for v in range(variables):
                gathered[t * variables + v, b * width : (b + 1) * width, :] = block[t, v]
    left = lambda u, v: mats[offset + u * variables + v]
    for t in range(count):
        faces = jnp.concatenate([gathered[t * variables + v] for v in range(variables)], axis=1)
        hats = jnp.dot(forward[...], faces, precision=precise, preferred_element_type=jnp.float32)
        hats = [hats[:, v * stations : (v + 1) * stations] for v in range(variables)]
        wave = []
        for u in range(variables):
            acc = left(u, 0) * hats[0]
            for v in range(1, variables):
                acc = acc + left(u, v) * hats[v]
            wave.append((acc[:rows], acc[rows:]))
        jumps = []
        for i in range(NI):
            cos_part = -tables[12] * wave[i][0]
            sin_part = -tables[12] * wave[i][1]
            for o in range(variables - NI):
                out_cos, out_sin = wave[NI + o]
                real, imag = tables[o * NI + i], tables[6 + o * NI + i]
                cos_part = cos_part + real * out_cos - imag * out_sin
                sin_part = sin_part + imag * out_cos + real * out_sin
            jumps.append(jnp.concatenate([cos_part, sin_part], axis=0))
        back = jnp.dot(
            backward[...], jnp.concatenate(jumps, axis=1), precision=precise, preferred_element_type=jnp.float32
        )
        for k, out in enumerate(outs):
            for i in range(NI):
                out[t, i] = back[k * cells : (k + 1) * cells, i * stations : (i + 1) * stations]


def whole_layer(pieces, place, planes):
    ordered = [jnp.where(place == 0, pieces[j], pieces[planes - 1 - j]) for j in range(planes)]
    return jnp.concatenate(ordered, axis=0)


def flux_kernel(mats, place, base, state, inv_volume, after, before, *rest, planes, neighbours, blocks, offset):
    faces, rest = rest[:planes], rest[planes:]
    layers, rest = rest[:neighbours], rest[neighbours:]
    jumps, out = rest[:blocks], rest[-1]
    variables, cells, stations = state.shape[1:]
    row = lax.broadcasted_iota(jnp.int32, (cells, stations), 0)
    volume = inv_volume[...]
    plane = place[0]
    first, last = plane == 0, plane == planes - 1
    face_sign = jnp.where(first, -0.5, 0.5)
    face_on = jnp.where(jnp.logical_or(first, last), 1.0, 0.0)
    if neighbours == 1:
        signs = [jnp.where(first, 0.5, -0.5)]
    else:
        signs = [0.5, -0.5]
    axial = lambda v, w, sign: sign * mats[v * variables + w] - (DISSIPATION if v == w else 0.0)
    face_mat = [[face_on * axial(v, w, face_sign) for w in range(variables)] for v in range(variables)]
    layer_mats = [[[axial(v, w, s) for w in range(variables)] for v in range(variables)] for s in signs]
    right = lambda v, i: mats[offset + v * variables + i]
    for k, jump in enumerate(jumps):
        start = place[1 + k]

        def step(n, carry, jump=jump, start=start):
            t = start + n
            half, total = [], []
            for w in range(variables):
                s = state[t, w]
                index = t * variables + w
                forward = jnp.where(row == cells - 1, after[pl.ds(index, 1), :], pltpu.roll(s, cells - 1, 0))
                backward = jnp.where(row == 0, before[pl.ds(index, 1), :], pltpu.roll(s, 1, 0))
                half.append(0.5 * (forward - backward))
                total.append(-DISSIPATION * (forward + backward))
            z = [jump[n, i] for i in range(NI)]
            layer = []
            for w in range(variables):
                face = whole_layer([f[t, w] for f in faces], plane, planes)
                layer.append(face + right(w, 0) * z[0] + right(w, 1) * z[1])
            for v in range(variables):
                acc = total[v]
                for w in range(variables):
                    acc = acc + mats[(variables + v) * variables + w] * half[w]
                    acc = acc + face_mat[v][w] * layer[w]
                    for mat, source in zip(layer_mats, layers):
                        acc = acc + mat[v][w] * source[t, w]
                out[t, v] = base[t, v] + volume * acc
            return carry

        lax.fori_loop(0, jump.shape[0], step, 0)


def corrected_kernel(mats, place, boundary, *rest, planes, blocks, offset):
    jumps, rest = rest[:blocks], rest[blocks:]
    backs, out = rest[:-1], rest[-1]
    variables, width = boundary.shape[2:4]
    plane = place[0]
    right = lambda v, i: mats[offset + v * variables + i]
    for k, jump in enumerate(jumps):
        start = place[1 + k]
        length = jump.shape[0]

        def step(n, carry, jump=jump, start=start, first=k * length):
            own = []
            for i in range(NI):
                value = jump[n, i, :width]
                for j in range(1, planes):
                    value = jnp.where(plane == j, jump[n, i, j * width : (j + 1) * width], value)
                own.append(value)
            for p in range(2):
                mine = plane == p * (planes - 1)
                for_p = []
                for i in range(NI):
                    value = backs[0][first + n, i]
                    for s in range(2, planes):
                        at = s if p == 0 else planes - 1 - s
                        value = jnp.where(plane == at, backs[s - 1][first + n, i], value)
                    for_p.append(jnp.where(mine, own[i], value))
                for v in range(variables):
                    out[start + n, p, v] = (
                        boundary[start + n, p, v] + right(v, 0) * for_p[0] + right(v, 1) * for_p[1]
                    )
            return carry

        lax.fori_loop(0, length, step, 0)


def call(kernel, shapes, smem, vmem, scratch=(), name=None):
    return pl.pallas_call(
        kernel,
        out_shape=shapes,
        in_specs=[SMEM_SPEC] * len(smem) + [VMEM_SPEC] * len(vmem),
        out_specs=jax.tree.map(lambda _: VMEM_SPEC, shapes),
        scratch_shapes=scratch,
        name=name,
    )(*smem, *vmem)


def local(
    state,
    boundary,
    inv_volume,
    flux_matrix,
    left_vectors,
    right_vectors,
    gain,
    harmonic_index,
    mode_count,
):
    f32 = jnp.float32
    tiles, planes, insts = lax.axis_size("tile"), lax.axis_size("plane"), lax.axis_size("inst")
    count, variables, _, cells, stations = state.shape
    width = boundary.shape[3]
    period = width * tiles * planes
    modes = gain.shape[2]
    tile, plane = lax.axis_index("tile"), lax.axis_index("plane")
    time_parts = math.gcd(count, tiles)
    lane_parts = tiles // time_parts
    length, lanes = count // time_parts, stations // lane_parts
    own_face = jnp.where(plane == 0, 0, 1)
    field = state.reshape(count, variables, cells, stations)

    def blocks_of(faces):
        split = faces.reshape(time_parts, length, variables, width, lane_parts, lanes)
        return lambda at: lax.dynamic_index_in_dim(
            lax.dynamic_index_in_dim(split, at // lane_parts, 0, keepdims=False), at % lane_parts, 3, keepdims=False
        )

    pieces = []
    for shift in range(1, planes):
        face = lax.dynamic_index_in_dim(boundary, jnp.where(plane == shift, 0, 1), 1, keepdims=False)
        pairs = [(shift, 0), (planes - 1 - shift, planes - 1)]
        pieces.append(lax.ppermute(face, "plane", pairs))
    pieces.insert(0, lax.dynamic_index_in_dim(boundary, own_face, 1, keepdims=False))

    takes = [blocks_of(piece) for piece in pieces]
    first_row = field[:, :, 0].reshape(count * variables, stations)
    last_row = field[:, :, cells - 1].reshape(count * variables, stations)
    even = tile % 2 == 0
    target = lambda step: partner(tile, step, tiles)[0]
    own_blocks, halos = [takes[0](tile)], {}
    for step in range(1, tiles):
        block = takes[0](target(step))
        own_blocks.append(lax.ppermute(block, "tile", tile_pairs(step, tiles)))
        if step in (1, tiles - 1):
            if tiles == 4:
                row = jnp.where(even == (step == 1), last_row, first_row)
            else:
                row = last_row if step == 1 else first_row
            halos[step] = lax.ppermute(row, "tile", tile_pairs(step, tiles))
    if tiles == 4:
        after = jnp.where(even, halos[1], halos[3])
        before = jnp.where(even, halos[3], halos[1])
    else:
        after, before = halos[tiles - 1], halos[1]

    others = [
        lax.ppermute(field, "inst", [((i + s) % insts, i) for i in range(insts)]) for s in range(1, insts)
    ]
    arrived = [own_blocks]
    for take in takes[1:]:
        arrived.append(
            [take(tile)]
            + [lax.ppermute(take(target(step)), "tile", tile_pairs(step, tiles)) for step in range(1, tiles)]
        )
    late, _ = lax.optimization_barrier((field, pieces[-1]))
    if planes == 2:
        layers = [lax.ppermute(late, "plane", [(0, 1), (1, 0)])]
    else:
        layers = [
            lax.ppermute(late, "plane", [(i + 1, i) for i in range(planes - 1)]),
            lax.ppermute(late, "plane", [(i, i + 1) for i in range(planes - 1)]),
        ]

    mats = jnp.concatenate([flux_matrix.reshape(-1), left_vectors.reshape(-1), right_vectors.reshape(-1)])
    left_at = 3 * variables * variables
    right_at = left_at + variables * variables
    fold, fold_sine, rows, class_count = fold_tables(modes, period)
    total = count * insts
    steps = np.arange(total)
    sine = np.sin(2.0 * np.pi * ((steps[:, None] * steps[None, :]) % total) / total) * (OMEGA_SCALE * 2.0 / total)
    forward, backward = cell_layouts(tiles, planes, width, rows, class_count)
    position = (tile * planes + plane) if tiles == 4 else plane
    forward = lax.dynamic_index_in_dim(jnp.asarray(forward), position, 0, keepdims=False)
    backward = lax.dynamic_index_in_dim(jnp.asarray(backward), position, 0, keepdims=False)
    face_gain = lax.dynamic_index_in_dim(gain, own_face, 0, keepdims=False)
    face_gain = jnp.transpose(face_gain, (0, 3, 2, 1)).reshape(-1, modes)
    station_modes = lax.dynamic_slice_in_dim(mode_count, own_face, 1, 0)
    station_modes = lax.dynamic_slice_in_dim(station_modes, (tile % lane_parts) * lanes, lanes, 1)

    base, tables = call(
        lambda *refs: base_kernel(*refs, inst_count=insts),
        (
            jax.ShapeDtypeStruct(field.shape, f32),
            jax.ShapeDtypeStruct((13, rows, lanes), f32),
        ),
        (mats, harmonic_index),
        (
            field,
            *others,
            inv_volume.reshape(cells, stations),
            jnp.asarray(sine, f32),
            face_gain,
            station_modes,
            jnp.asarray(fold),
            jnp.asarray(fold_sine),
        ),
        [pltpu.VMEM((total, stations), f32)],
        name="base",
    )

    jumps = call(
        lambda *refs: jump_kernel(*refs, tiles=tiles, planes=planes, offset=left_at),
        tuple(jax.ShapeDtypeStruct((length, NI, cells, lanes), f32) for _ in range(tiles)),
        (mats,),
        (forward, backward, tables, *[arrived[shift][step] for step in range(tiles) for shift in range(planes)]),
        [pltpu.VMEM((length * variables, period, lanes), f32)],
        name="jump",
    )
    jumps = [jumps[0]] + [
        lax.ppermute(jumps[step], "tile", tile_pairs(step, tiles)) for step in range(1, tiles)
    ]
    sources = np.array([[partner(i, s, tiles)[1] for s in range(tiles)] for i in range(tiles)])
    if lane_parts == 1:
        starts = sources * length
    else:
        order = jnp.asarray(np.argsort(sources, axis=1))[tile]
        whole = jnp.take(jnp.stack(jumps), order, axis=0)
        whole = whole.reshape(time_parts, lane_parts, length, NI, cells, lanes)
        whole = jnp.transpose(whole, (0, 2, 3, 4, 1, 5)).reshape(count, NI, cells, stations)
        jumps = [whole]
        starts = np.zeros((tiles, 1), np.int64)
    places = np.array(
        [[p] + list(starts[t]) for t in range(tiles) for p in range(planes)], np.int32
    )
    place = lax.dynamic_index_in_dim(jnp.asarray(places), tile * planes + plane, 0, keepdims=False)

    backs = []
    for shift in range(1, planes):
        at = jnp.where(plane == 0, shift, planes - 1 - shift)
        part = jnp.concatenate(
            [lax.dynamic_slice_in_dim(jump, at * width, width, 2) for jump in jumps], axis=0
        )
        backs.append(lax.ppermute(part, "plane", [(0, shift), (planes - 1, planes - 1 - shift)]))

    residual = call(
        lambda *refs: flux_kernel(
            *refs, planes=planes, neighbours=len(layers), blocks=len(jumps), offset=right_at
        ),
        jax.ShapeDtypeStruct(field.shape, f32),
        (mats, place),
        (base, field, inv_volume.reshape(cells, stations), after, before, *pieces, *layers, *jumps),
        name="flux",
    )
    corrected = call(
        lambda *refs: corrected_kernel(*refs, planes=planes, blocks=len(jumps), offset=right_at),
        jax.ShapeDtypeStruct(boundary.shape, f32),
        (mats, place),
        (boundary, *jumps, *backs),
        name="corrected",
    )
    return (residual.reshape(state.shape), corrected)


def solution(mesh):
    return jax.shard_map(
        local,
        mesh=mesh,
        in_specs=(
            P("inst", "groups", "plane", "tile", None),
            P("inst", None, "groups", ("tile", "plane"), None),
            P(("groups", "plane"), "tile", None),
            P("groups", None, None),
            P("groups", None),
            P("groups", None),
            P("groups", None, None, None, None),
            P("groups"),
            P("groups", None),
        ),
        out_specs=(
            P("inst", "groups", "plane", "tile", None),
            P("inst", None, "groups", ("tile", "plane"), None),
        ),
        check_vma=False,
    )
```

```python
import math

import jax
import jax.numpy as jnp
import numpy as np
from jax import lax
from jax.experimental import pallas as pl
from jax.experimental.pallas import tpu as pltpu
from jax.sharding import PartitionSpec as P


NI = 2
DISSIPATION = 0.25
OMEGA_SCALE = 0.1
KERNEL_VMEM = 6 << 20
precise = lax.Precision.HIGHEST
VMEM_SPEC = pl.BlockSpec(memory_space=pltpu.VMEM)
SMEM_SPEC = pl.BlockSpec(memory_space=pltpu.SMEM)


def partner(position, step, count):
    if count == 4:
        return position ^ step, position ^ step
    return (position + step) % count, (position - step) % count


def tile_pairs(step, count):
    return [(i, partner(i, step, count)[0]) for i in range(count)]


def mode_classes(mode_total, period):
    residue = np.arange(mode_total) % period
    classes = np.minimum(residue, period - residue)
    signs = np.where(residue <= period - residue, 1.0, -1.0)
    return classes, signs, min(mode_total, period // 2 + 1)


def fold_tables(mode_total, period):
    classes, signs, count = mode_classes(mode_total, period)
    rows = -(-count // 8) * 8
    fold = np.zeros((rows, mode_total), np.float32)
    fold[classes, np.arange(mode_total)] = 1.0
    return fold, fold * signs.astype(np.float32)[None, :], rows, count


def class_waves(cells, rows, count, period):
    out = np.zeros((2 * rows, len(cells)))
    phase = 2.0 * np.pi * ((np.arange(count)[:, None] * np.asarray(cells)[None, :]) % period) / period
    out[:count] = np.cos(phase)
    out[rows : rows + count] = np.sin(phase)
    return out


def rate_waves(count, total, cells):
    half = total // 2 + 1
    half = -(-half // 8) * 8
    angle = lambda steps: 2.0 * np.pi * ((np.asarray(steps)[:, None] * np.arange(half)[None, :]) % total) / total
    live = (np.arange(half) < (total + 1) // 2).astype(np.float64)[None, :]
    rows, columns = angle(np.arange(count)), angle(np.arange(total))
    out = np.concatenate([np.cos(rows) * live, -np.sin(rows) * live], axis=1) * (OMEGA_SCALE * 2.0 / total)
    into = np.concatenate([np.sin(columns), np.cos(columns)], axis=1).T
    return np.repeat(out, cells, axis=0).astype(np.float32), np.repeat(into, cells, axis=1).astype(np.float32)


def cell_layouts(tiles, planes, face_cells, rows, count):
    cells, period = planes * face_cells, tiles * planes * face_cells
    positions = tiles if tiles == 4 else 1
    forward = np.zeros((positions * planes, 2 * rows, period), np.float32)
    backward = np.zeros((positions * planes, period, 2 * rows), np.float32)
    for position in range(positions):
        for plane in range(planes):
            arrive, depart = [], []
            for step in range(tiles):
                target, source = partner(position, step, tiles)
                for shift in range(planes):
                    other = face_plane(plane, shift, planes)
                    arrive += [source * cells + other * face_cells + k for k in range(face_cells)]
                depart += [target * cells + k for k in range(cells)]
            forward[position * planes + plane] = class_waves(arrive, rows, count, period) * (2.0 / period)
            backward[position * planes + plane] = class_waves(depart, rows, count, period).T
    return forward, backward


def face_plane(plane, shift, planes):
    if shift == 0:
        return plane
    return shift if plane == 0 else planes - 1 - shift


def place():
    return lax.axis_index("tile"), lax.axis_index("plane")


def split_rows(x):
    high = x.astype(jnp.bfloat16)
    return high, (x - high.astype(jnp.float32)).astype(jnp.bfloat16)


def split_dot(a, b):
    a_high, a_low = split_rows(a)
    b_high, b_low = split_rows(b)
    left = jnp.concatenate([a_high, a_high, a_low], axis=1)
    right = jnp.concatenate([b_high, b_low, b_high], axis=0)
    return jnp.dot(left, right, preferred_element_type=jnp.float32)


def run_copies(copies, sems):
    started = [pltpu.make_async_copy(source, target, sems.at[k]) for k, (source, target) in enumerate(copies)]
    for copy in started:
        copy.start()
    for copy in started:
        copy.wait()


def face_message_kernel(boundary, out, sems, *, shift, tiles):
    tile, plane = place()
    face = jnp.where(plane == shift, 0, 1)
    length = out.shape[1]
    copies = []
    for step in range(tiles):
        start = partner(tile, step, tiles)[0] * length
        copies.append((boundary.at[pl.ds(start, length), face], out.at[step]))
    run_copies(copies, sems)


def own_message_kernel(boundary, *rest, tiles):
    outs, sems = rest[:-1], rest[-1]
    tile, plane = place()
    face = jnp.where(plane == 0, 0, 1)
    length = outs[0].shape[0]
    copies = []
    for step, out in enumerate(outs):
        start = partner(tile, step, tiles)[0] * length
        copies.append((boundary.at[pl.ds(start, length), face], out))
    run_copies(copies, sems)


def table_kernel(gain, station_modes, fold, fold_sine, tables):
    modes = fold.shape[1]
    mode = lax.broadcasted_iota(jnp.int32, (modes, station_modes.shape[1]), 0)
    resolved = (mode < station_modes[...]).astype(jnp.float32)
    rows = fold.shape[0]
    parts = [fold[...] * gain[k : k + 1, :] for k in range(6)]
    parts += [fold_sine[...] * gain[k : k + 1, :] for k in range(6, 12)]
    parts.append(fold[...])
    summed = jnp.dot(jnp.concatenate(parts, axis=0), resolved, precision=precise, preferred_element_type=jnp.float32)
    for k in range(13):
        tables[k] = summed[k * rows : (k + 1) * rows]


def rate_kernel(fluxes, harmonics, state, *rest, inst_count):
    others = rest[: inst_count - 1]
    inv_volume, out_waves, in_waves, out, rates = rest[inst_count - 1 :]
    local_count, variables, cells, stations = state.shape
    total = local_count * inst_count
    width = out_waves.shape[1]
    half_width = width // 2
    lane = lax.broadcasted_iota(jnp.int32, (1, width), 1)
    lane = jnp.where(lane < half_width, lane, lane - half_width)
    present = jnp.zeros((1, width), jnp.float32)
    for k in range(harmonics.shape[0]):
        h = harmonics[k]
        residue = lax.rem(h, total)
        weight = h.astype(jnp.float32)
        present = present + jnp.where(lane == residue, weight, 0.0) - jnp.where(lane == total - residue, weight, 0.0)
    count = local_count * cells
    matrix = split_dot(out_waves[...] * present, in_waves[...])
    rows = lax.broadcasted_iota(jnp.int32, matrix.shape, 0)
    columns = lax.broadcasted_iota(jnp.int32, matrix.shape, 1)
    matrix = jnp.where(lax.rem(rows, cells) == lax.rem(columns, cells), matrix, 0.0)
    high, low = split_rows(matrix)
    left = jnp.concatenate([high, high, low], axis=1)
    for v in range(variables):
        flat = jnp.concatenate(
            [source[:, v].reshape(count, stations) for source in (state,) + tuple(others)], axis=0
        )
        b_high, b_low = split_rows(flat)
        right = jnp.concatenate([b_high, b_low, b_high], axis=0)
        rates[v] = jnp.dot(left, right, preferred_element_type=jnp.float32).reshape(local_count, cells, stations)
    lanes = lax.broadcasted_iota(jnp.int32, (cells, stations), 1)
    volume = inv_volume[...]

    def radial_of(t, carry):
        half, total_of = [], []
        for w in range(variables):
            s = state[t, w]
            forward = jnp.where(lanes == stations - 1, 0.0, pltpu.roll(s, stations - 1, 1))
            backward = jnp.where(lanes == 0, 0.0, pltpu.roll(s, 1, 1))
            half.append(0.5 * (forward - backward))
            total_of.append((6.0 * DISSIPATION) * s - DISSIPATION * (forward + backward))
        for v in range(variables):
            acc = total_of[v]
            for w in range(variables):
                acc = acc + fluxes[(2 * variables + v) * variables + w] * half[w]
            out[t, v] = rates[v, t] + volume * acc
        return carry

    lax.fori_loop(0, local_count, radial_of, 0)


def jump_kernel(lefts, forward, backward, tables, *rest, tiles, planes):
    blocks = rest[: tiles * planes]
    outs = rest[tiles * planes : tiles * planes + tiles]
    gathered = rest[-1]
    count, variables, width, stations = blocks[0].shape
    rows = tables.shape[1]
    cells = outs[0].shape[2]
    count = outs[0].shape[0]
    for b, block in enumerate(blocks):
        for t in range(count):
            for v in range(variables):
                gathered[t * variables + v, b * width : (b + 1) * width, :] = block[t, v]
    left = lambda u, v: lefts[u * variables + v]
    tile, plane = place()
    position = tile * planes + plane if forward.shape[0] > planes else plane
    into, back_from = forward[position], backward[position]
    for t in range(count):
        faces = jnp.concatenate([gathered[t * variables + v] for v in range(variables)], axis=1)
        hats = split_dot(into, faces)
        hats = [hats[:, v * stations : (v + 1) * stations] for v in range(variables)]
        wave = []
        for u in range(variables):
            acc = left(u, 0) * hats[0]
            for v in range(1, variables):
                acc = acc + left(u, v) * hats[v]
            wave.append((acc[:rows], acc[rows:]))
        jumps = []
        for i in range(NI):
            cos_part = -tables[12] * wave[i][0]
            sin_part = -tables[12] * wave[i][1]
            for o in range(variables - NI):
                out_cos, out_sin = wave[NI + o]
                real, imag = tables[o * NI + i], tables[6 + o * NI + i]
                cos_part = cos_part + real * out_cos - imag * out_sin
                sin_part = sin_part + imag * out_cos + real * out_sin
            jumps.append(jnp.concatenate([cos_part, sin_part], axis=0))
        back = split_dot(back_from, jnp.concatenate(jumps, axis=1))
        for k, out in enumerate(outs):
            for i in range(NI):
                out[t, i] = back[k * cells : (k + 1) * cells, i * stations : (i + 1) * stations]


def block_start(tile, k, blocks, length):
    return partner(tile, k, blocks)[1] * length if blocks > 1 else 0


def axial_sign(plane):
    return jnp.where(plane == 0, -0.5, 0.5)


def flux_kernel(fluxes, base, state, inv_volume, *rest, planes, tiles, neighbours):
    halos, rest = rest[:2], rest[2:]
    pieces, rest = rest[: planes - 1], rest[planes - 1 :]
    layers, rest = rest[:neighbours], rest[neighbours:]
    own, out = rest[:-1], rest[-1]
    variables, cells, stations = state.shape[1:]
    row = lax.broadcasted_iota(jnp.int32, (cells, stations), 0)
    volume = inv_volume[...]
    tile, plane = place()
    face_on = jnp.where(jnp.logical_or(plane == 0, plane == planes - 1), 1.0, 0.0)
    signs = [-axial_sign(plane)] if neighbours == 1 else [0.5, -0.5]
    axial = lambda v, w, sign: sign * fluxes[v * variables + w] - (DISSIPATION if v == w else 0.0)
    face_mat = [[face_on * axial(v, w, axial_sign(plane)) for w in range(variables)] for v in range(variables)]
    layer_mats = [[[axial(v, w, s) for w in range(variables)] for v in range(variables)] for s in signs]
    swapped = tile % 2 == 1 if tiles == 4 else None
    blocks = pieces[0].shape[0]
    length = pieces[0].shape[1]
    for k in range(blocks):
        start = block_start(tile, k, blocks, length)

        def step(n, carry, k=k, start=start):
            t = start + n
            half, total, layer = [], [], []
            for w in range(variables):
                s = state[t, w]
                first, second = halos[0][t, w], halos[1][t, w]
                if swapped is not None:
                    first, second = jnp.where(swapped, second, first), jnp.where(swapped, first, second)
                forward = jnp.where(row == cells - 1, first, pltpu.roll(s, cells - 1, 0))
                backward = jnp.where(row == 0, second, pltpu.roll(s, 1, 0))
                half.append(0.5 * (forward - backward))
                total.append(-DISSIPATION * (forward + backward))
                parts = [own[mirror(k, blocks)][n, w]] + [piece[k, n, w] for piece in pieces]
                ordered = [jnp.where(plane == 0, parts[j], parts[planes - 1 - j]) for j in range(planes)]
                layer.append(jnp.concatenate(ordered, axis=0))
            for v in range(variables):
                acc = total[v]
                for w in range(variables):
                    acc = acc + fluxes[(variables + v) * variables + w] * half[w]
                    acc = acc + face_mat[v][w] * layer[w]
                    for mat, source in zip(layer_mats, layers):
                        acc = acc + mat[v][w] * source[t, w]
                out[t, v] = base[t, v] + volume * acc
            return carry

        lax.fori_loop(0, length, step, 0)


def finish_kernel(fluxes, rights, base, inv_volume, *rest, planes, blocks):
    jumps, rest = rest[:blocks], rest[blocks:]
    own, (out, corrected, field, own_face, sems) = rest[:blocks], rest[blocks:]
    variables, width = own[0].shape[1:3]
    volume = inv_volume[...]
    tile, plane = place()
    face = jnp.where(plane == 0, 0, 1)
    face_on = jnp.where(jnp.logical_or(plane == 0, plane == planes - 1), 1.0, 0.0)
    right = [[rights[v * variables + i] for i in range(NI)] for v in range(variables)]
    sign = axial_sign(plane)
    mixed = []
    for v in range(variables):
        mixed.append([])
        for i in range(NI):
            acc = -DISSIPATION * right[v][i]
            for w in range(variables):
                acc = acc + sign * fluxes[v * variables + w] * right[w][i]
            mixed[v].append(face_on * acc)
    length = jumps[0].shape[0]
    copies = []
    for k, jump in enumerate(jumps):
        start = block_start(tile, k, blocks, length)
        faces = own[mirror(k, blocks)]

        def step(n, carry, jump=jump, start=start, faces=faces):
            t = start + n
            z = [jump[n, i] for i in range(NI)]
            values = []
            for i in range(NI):
                value = z[i][:width]
                for j in range(1, planes):
                    value = jnp.where(plane == j, z[i][j * width : (j + 1) * width], value)
                values.append(value)
            for v in range(variables):
                field[t, v] = base[t, v] + volume * (mixed[v][0] * z[0] + mixed[v][1] * z[1])
                own_face[t, v] = faces[n, v] + right[v][0] * values[0] + right[v][1] * values[1]
            return carry

        lax.fori_loop(0, length, step, 0)
        part = pl.ds(start, length)
        copies.append(pltpu.make_async_copy(field.at[part], out.at[part], sems.at[2 * k]))
        copies.append(pltpu.make_async_copy(own_face.at[part], corrected.at[part, face], sems.at[2 * k + 1]))
        copies[-2].start()
        copies[-1].start()
    for copy in copies:
        copy.wait()


def back_kernel(*refs, shift, planes):
    jumps, out = refs[:-1], refs[-1]
    _, plane = place()
    at = jnp.where(plane == 0, shift, planes - 1 - shift)
    length, _, width, _ = out.shape
    length = length // len(jumps)
    for k, jump in enumerate(jumps):
        for n in range(length):
            for i in range(NI):
                z = jump[n, i]
                value = z[:width]
                for j in range(1, planes):
                    value = jnp.where(at == j, z[j * width : (j + 1) * width], value)
                out[k * length + n, i] = value


def other_kernel(rights, *rest, planes, blocks):
    backs, rest = rest[: planes - 1], rest[planes - 1 :]
    faces, (partial, corrected, values, sems) = rest[:-4], rest[-4:]
    variables = faces[0].shape[-3]
    tile, plane = place()
    right = [[rights[v * variables + i] for i in range(NI)] for v in range(variables)]
    length = backs[0].shape[0] // blocks
    if planes == 2:
        copies = []
        for k in range(blocks):
            start = block_start(tile, k, blocks, length)

            def step(n, carry, k=k, start=start):
                z = [backs[0][k * length + n, i] for i in range(NI)]
                for v in range(variables):
                    values[0, start + n, v] = (
                        faces[0][mirror(k, blocks), n, v] + right[v][0] * z[0] + right[v][1] * z[1]
                    )
                return carry

            lax.fori_loop(0, length, step, 0)
            part = pl.ds(start, length)
            other = jnp.where(plane == 0, 1, 0)
            copies.append(pltpu.make_async_copy(values.at[0, part], corrected.at[part, other], sems.at[k]))
            copies[-1].start()
        for copy in copies:
            copy.wait()
        return
    for p in range(2):

        @pl.when(plane != p * (planes - 1))
        def _():
            for k in range(blocks):
                start = block_start(tile, k, blocks, length)

                def step(n, carry, k=k, start=start):
                    z = []
                    for i in range(NI):
                        value = backs[0][k * length + n, i]
                        for s in range(2, planes):
                            at = s if p == 0 else planes - 1 - s
                            value = jnp.where(plane == at, backs[s - 1][k * length + n, i], value)
                        z.append(value)
                    for v in range(variables):
                        values[p, start + n, v] = (
                            faces[0][start + n, p, v] + right[v][0] * z[0] + right[v][1] * z[1]
                        )
                    return carry

                lax.fori_loop(0, length, step, 0)
            copy = pltpu.make_async_copy(values.at[p], corrected.at[:, p], sems.at[p])
            copy.start()
            copy.wait()


def load_kernel(state, field, *rest, tiles):
    rows, sem = rest[:-1], rest[-1]
    copy = pltpu.make_async_copy(state, field, sem)
    copy.start()
    copy.wait()
    tile, _ = place()
    count, variables, cells, _ = field.shape
    even = tile % 2 == 0
    for k, out in enumerate(rows):
        ahead = even == (k == 0) if tiles == 4 else k == 0

        def step(t, carry, out=out, ahead=ahead):
            for v in range(variables):
                out[t, v] = jnp.where(ahead, field[t, v, cells - 1 :], field[t, v, :1])
            return carry

        lax.fori_loop(0, count, step, 0)


def mirror(k, blocks):
    return k if blocks in (1, 4) else (blocks - k) % blocks


ANY_SPEC = pl.BlockSpec(memory_space=pl.ANY)


def call(kernel, shapes, smem, arrays, scratch=(), hbm=(), final={}, aliases=None):
    arrays = [a if i in hbm else pltpu.with_memory_space_constraint(a, pltpu.VMEM) for i, a in enumerate(arrays)]
    return pl.pallas_call(
        kernel,
        out_shape=[s if i in final else pltpu.VMEM(s.shape, s.dtype) for i, s in enumerate(shapes)],
        in_specs=[SMEM_SPEC] * len(smem) + [ANY_SPEC if i in hbm else VMEM_SPEC for i in range(len(arrays))],
        out_specs=[final[i] if i in final else VMEM_SPEC for i in range(len(shapes))],
        scratch_shapes=scratch,
        input_output_aliases=aliases or {},
        compiler_params=pltpu.CompilerParams(vmem_limit_bytes=KERNEL_VMEM),
    )(*smem, *arrays)


def local(
    state,
    boundary,
    inv_volume,
    flux_matrix,
    left_vectors,
    right_vectors,
    gain,
    harmonic_index,
    mode_count,
):
    f32 = jnp.float32
    tiles, planes, insts = lax.axis_size("tile"), lax.axis_size("plane"), lax.axis_size("inst")
    count, variables, _, cells, stations = state.shape
    width = boundary.shape[3]
    period = width * tiles * planes
    modes = gain.shape[2]
    tile, plane = lax.axis_index("tile"), lax.axis_index("plane")
    time_parts = math.gcd(count, tiles)
    lane_parts = tiles // time_parts
    length, lanes = count // time_parts, stations // lane_parts
    own_face = jnp.where(plane == 0, 0, 1)
    field = state.reshape(count, variables, cells, stations)
    struct = lambda *shape: jax.ShapeDtypeStruct(shape, f32)
    by_kernel = lane_parts == 1
    blocks = tiles if by_kernel else 1

    def blocks_of(faces):
        split = faces.reshape(time_parts, length, variables, width, lane_parts, lanes)
        return lambda at: lax.dynamic_index_in_dim(
            lax.dynamic_index_in_dim(split, at // lane_parts, 0, keepdims=False), at % lane_parts, 3, keepdims=False
        )

    target = lambda step: partner(tile, step, tiles)[0]

    pieces, messages = [], []
    for shift in range(1, planes):
        pairs = [(shift, 0), (planes - 1 - shift, planes - 1)]
        if by_kernel:
            message = call(
                lambda *refs: face_message_kernel(*refs, shift=shift, tiles=tiles),
                [struct(tiles, length, variables, width, stations)],
                (),
                (boundary,),
                [pltpu.SemaphoreType.DMA((tiles,))],
                hbm=(0,),
            )[0]
        else:
            message = lax.dynamic_index_in_dim(boundary, jnp.where(plane == shift, 0, 1), 1, keepdims=False)
            message = message[None]
        messages.append(message)
        pieces.append(lax.ppermute(message, "plane", pairs))

    if by_kernel:
        own_blocks = call(
            lambda *refs: own_message_kernel(*refs, tiles=tiles),
            [struct(length, variables, width, stations)] * tiles,
            (),
            (boundary,),
            [pltpu.SemaphoreType.DMA((tiles,))],
            hbm=(0,),
        )
        takes = [lambda step, piece=piece: piece[step] for piece in pieces]
    else:
        take_own = blocks_of(lax.dynamic_index_in_dim(boundary, own_face, 1, keepdims=False))
        own_blocks = [take_own(target(step)) for step in range(tiles)]
        takes = [lambda step, take=blocks_of(piece[0]): take(target(step)) for piece in pieces]
    order = list(range(tiles - 1, 0, -1))
    own_arrived = {0: own_blocks[0]}
    for step in order:
        own_arrived[step] = lax.ppermute(own_blocks[step], "tile", tile_pairs(step, tiles))
    field, *rows_out = call(
        lambda *refs: load_kernel(*refs, tiles=tiles),
        [struct(*field.shape)] + [struct(count, variables, 1, stations)] * 2,
        (),
        (field,),
        [pltpu.SemaphoreType.DMA(())],
        hbm=(0,),
    )
    others = [lax.ppermute(field, "inst", [((i + s) % insts, i) for i in range(insts)]) for s in range(1, insts)]
    arrived = [own_arrived]
    for shift, take in enumerate(takes):
        got = {0: take(0)}
        for step in order:
            got[step] = lax.ppermute(take(step), "tile", tile_pairs(step, tiles))
        arrived.append(got)
    if planes == 2:
        layers = [lax.ppermute(field, "plane", [(0, 1), (1, 0)])]
    else:
        layers = [
            lax.ppermute(field, "plane", [(i + 1, i) for i in range(planes - 1)]),
            lax.ppermute(field, "plane", [(i, i + 1) for i in range(planes - 1)]),
        ]
    halos = [lax.ppermute(row, "tile", tile_pairs(step, tiles)) for row, step in zip(rows_out, (1, tiles - 1))]
    if tiles != 4:
        halos = halos[::-1]

    fluxes, lefts, rights = flux_matrix.reshape(-1), left_vectors.reshape(-1), right_vectors.reshape(-1)
    fold, fold_sine, rows, class_count = fold_tables(modes, period)
    total = count * insts
    out_waves, in_waves = rate_waves(count, total, cells)
    forward, backward = cell_layouts(tiles, planes, width, rows, class_count)
    face_gain = lax.dynamic_index_in_dim(gain, own_face, 0, keepdims=False)
    face_gain = jnp.transpose(face_gain, (0, 3, 2, 1)).reshape(-1, modes)
    station_modes = lax.dynamic_slice_in_dim(mode_count, own_face, 1, 0)
    station_modes = lax.dynamic_slice_in_dim(station_modes, (tile % lane_parts) * lanes, lanes, 1)
    volume = inv_volume.reshape(cells, stations)

    tables = call(
        table_kernel,
        [struct(13, rows, lanes)],
        (),
        (face_gain, station_modes, jnp.asarray(fold), jnp.asarray(fold_sine)),
    )[0]
    base = call(
        lambda *refs: rate_kernel(*refs, inst_count=insts),
        [struct(*field.shape)],
        (fluxes, harmonic_index),
        (field, *others, volume, jnp.asarray(out_waves), jnp.asarray(in_waves)),
        [pltpu.VMEM((variables, count, cells, stations), f32)],
    )[0]
    jumps = call(
        lambda *refs: jump_kernel(*refs, tiles=tiles, planes=planes),
        [struct(length, NI, cells, lanes)] * tiles,
        (lefts,),
        (jnp.asarray(forward), jnp.asarray(backward), tables, *[arrived[shift][step] for step in range(tiles) for shift in range(planes)]),
        [pltpu.VMEM((length * variables, period, lanes), f32)],
    )
    came = {0: jumps[0]}
    for step in order:
        came[step] = lax.ppermute(jumps[step], "tile", tile_pairs(step, tiles))
    jumps = [came[step] for step in range(tiles)]
    if not by_kernel:
        sources = np.array([[partner(i, s, tiles)[1] for s in range(tiles)] for i in range(tiles)])
        places = jnp.asarray(np.argsort(sources, axis=1))[tile]
        whole = jnp.take(jnp.stack(jumps), places, axis=0)
        whole = whole.reshape(time_parts, lane_parts, length, NI, cells, lanes)
        jumps = [jnp.transpose(whole, (0, 2, 3, 4, 1, 5)).reshape(count, NI, cells, stations)]

    if by_kernel:
        own_faces, other_faces = own_blocks, [messages[0]] if planes == 2 else [boundary]
    else:
        own_faces = [lax.dynamic_index_in_dim(boundary, own_face, 1, keepdims=False)]
        other_faces = [messages[0] if planes == 2 else boundary]
    backs = []
    for shift in range(1, planes):
        part = call(
            lambda *refs: back_kernel(*refs, shift=shift, planes=planes),
            [struct(count, NI, width, stations)],
            (),
            tuple(jumps),
        )[0]
        backs.append(lax.ppermute(part, "plane", [(0, shift), (planes - 1, planes - 1 - shift)]))

    inner = call(
        lambda *refs: flux_kernel(*refs, planes=planes, tiles=tiles, neighbours=len(layers)),
        [struct(*field.shape)],
        (fluxes,),
        (base, field, volume, *halos, *pieces, *layers, *own_faces),
    )[0]
    residual, partial = call(
        lambda *refs: finish_kernel(*refs, planes=planes, blocks=blocks),
        [struct(*field.shape), struct(*boundary.shape)],
        (fluxes, rights),
        (inner, volume, *jumps, *own_faces),
        [
            pltpu.VMEM(field.shape, f32),
            pltpu.VMEM((count, variables, width, stations), f32),
            pltpu.SemaphoreType.DMA((2 * blocks,)),
        ],
        final={0: ANY_SPEC, 1: ANY_SPEC},
    )
    corrected = call(
        lambda *refs: other_kernel(*refs, planes=planes, blocks=blocks),
        [struct(*boundary.shape)],
        (rights,),
        (*backs, *other_faces, partial),
        [
            pltpu.VMEM((1 if planes == 2 else 2, count, variables, width, stations), f32),
            pltpu.SemaphoreType.DMA((max(blocks, 2),)),
        ],
        hbm=(planes,),
        final={0: ANY_SPEC},
        aliases={planes + 1: 0},
    )[0]
    return (residual.reshape(state.shape), corrected)


def solution(mesh):
    return jax.shard_map(
        local,
        mesh=mesh,
        in_specs=(
            P("inst", "groups", "plane", "tile", None),
            P("inst", None, "groups", ("tile", "plane"), None),
            P(("groups", "plane"), "tile", None),
            P("groups", None, None),
            P("groups", None),
            P("groups", None),
            P("groups", None, None, None, None),
            P("groups"),
            P("groups", None),
        ),
        out_specs=(
            P("inst", "groups", "plane", "tile", None),
            P("inst", None, "groups", ("tile", "plane"), None),
        ),
        check_vma=False,
    )
```

```python
import math

import jax
import jax.numpy as jnp
import numpy as np
from jax import lax
from jax.experimental import pallas as pl
from jax.experimental.pallas import tpu as pltpu
from jax.sharding import PartitionSpec as P


NI = 2
DISSIPATION = 0.25
OMEGA_SCALE = 0.1
KERNEL_VMEM = 8 << 20
UNROLL = 6
FACE_GROUPS = [[2, 1], [0, 3]]
EARLY = 3
precise = lax.Precision.HIGHEST
VMEM_SPEC = pl.BlockSpec(memory_space=pltpu.VMEM)
SMEM_SPEC = pl.BlockSpec(memory_space=pltpu.SMEM)


def partner(position, step, count):
    if count == 4:
        return position ^ step, position ^ step
    return (position + step) % count, (position - step) % count


def tile_pairs(step, count):
    return [(i, partner(i, step, count)[0]) for i in range(count)]


def mode_classes(mode_total, period):
    residue = np.arange(mode_total) % period
    classes = np.minimum(residue, period - residue)
    signs = np.where(residue <= period - residue, 1.0, -1.0)
    return classes, signs, min(mode_total, period // 2 + 1)


def fold_tables(mode_total, period):
    classes, signs, count = mode_classes(mode_total, period)
    rows = -(-count // 8) * 8
    fold = np.zeros((rows, mode_total), np.float32)
    fold[classes, np.arange(mode_total)] = 1.0
    return fold, fold * signs.astype(np.float32)[None, :], rows, count


def class_waves(cells, rows, count, period):
    out = np.zeros((2 * rows, len(cells)))
    phase = 2.0 * np.pi * ((np.arange(count)[:, None] * np.asarray(cells)[None, :]) % period) / period
    out[:count] = np.cos(phase)
    out[rows : rows + count] = np.sin(phase)
    return out


def rate_waves(count, total, cells):
    half = total // 2 + 1
    half = -(-half // 8) * 8
    angle = lambda steps: 2.0 * np.pi * ((np.asarray(steps)[:, None] * np.arange(half)[None, :]) % total) / total
    live = (np.arange(half) < (total + 1) // 2).astype(np.float64)[None, :]
    rows, columns = angle(np.arange(count)), angle(np.arange(total))
    out = np.concatenate([np.cos(rows) * live, -np.sin(rows) * live], axis=1) * (OMEGA_SCALE * 2.0 / total)
    into = np.concatenate([np.sin(columns), np.cos(columns)], axis=1).T
    return np.repeat(out, cells, axis=0).astype(np.float32), np.repeat(into, cells, axis=1).astype(np.float32)


def cell_layouts(tiles, planes, face_cells, rows, count):
    cells, period = planes * face_cells, tiles * planes * face_cells
    positions = tiles if tiles == 4 else 1
    forward = np.zeros((positions * planes, 2 * rows, period), np.float32)
    backward = np.zeros((positions * planes, period, 2 * rows), np.float32)
    for position in range(positions):
        for plane in range(planes):
            arrive, depart = [], []
            for step in range(tiles):
                target, source = partner(position, step, tiles)
                for shift in range(planes):
                    other = face_plane(plane, shift, planes)
                    arrive += [source * cells + other * face_cells + k for k in range(face_cells)]
                depart += [target * cells + k for k in range(cells)]
            forward[position * planes + plane] = class_waves(arrive, rows, count, period) * (2.0 / period)
            backward[position * planes + plane] = class_waves(depart, rows, count, period).T
    return forward, backward


def face_plane(plane, shift, planes):
    if shift == 0:
        return plane
    return shift if plane == 0 else planes - 1 - shift


def place():
    return lax.axis_index("tile"), lax.axis_index("plane")


def split_rows(x):
    high = x.astype(jnp.bfloat16)
    return high, (x - high.astype(jnp.float32)).astype(jnp.bfloat16)


def split_dot(a, b):
    a_high, a_low = split_rows(a)
    b_high, b_low = split_rows(b)
    left = jnp.concatenate([a_high, a_high, a_low], axis=1)
    right = jnp.concatenate([b_high, b_low, b_high], axis=0)
    return jnp.dot(left, right, preferred_element_type=jnp.float32)


def face_message_kernel(boundary, *outs, groups, shift, tiles):
    tile, plane = place()
    face = jnp.where(plane == shift, 0, 1)
    length, variables = outs[0].shape[1:3]
    for steps, out in zip(groups, outs):
        for k, step in enumerate(steps):
            start = partner(tile, step, tiles)[0] * length
            for n in range(length):
                for v in range(variables):
                    out[k, n, v] = boundary[start + n, face, v]


def own_message_kernel(boundary, *outs, steps, tiles):
    tile, plane = place()
    face = jnp.where(plane == 0, 0, 1)
    length, variables = outs[0].shape[:2]
    for step, out in zip(steps, outs):
        start = partner(tile, step, tiles)[0] * length
        for n in range(length):
            for v in range(variables):
                out[n, v] = boundary[start + n, face, v]


def halo_message_kernel(state, *outs, tiles):
    halves, outs = outs[2:], outs[:2]
    halves[0][...] = state[: halves[0].shape[0]]
    halves[1][...] = state[halves[0].shape[0] :]
    tile, _ = place()
    count, variables, cells, _ = state.shape
    even = tile % 2 == 0
    for k, out in enumerate(outs):
        ahead = even == (k == 0) if tiles == 4 else k == 0
        for t in range(count):
            for v in range(variables):
                row = t * variables + v
                out[row // cells, row % cells : row % cells + 1] = jnp.where(
                    ahead, state[t, v, cells - 1 :], state[t, v, :1]
                )


def early_message_kernel(boundary, out, sem, *, step, tiles):
    tile, _ = place()
    length = out.shape[0]
    copy = pltpu.make_async_copy(boundary.at[pl.ds(partner(tile, step, tiles)[0] * length, length)], out, sem)
    copy.start()
    copy.wait()


def swap_message_kernel(block, out):
    _, plane = place()
    length, _, variables = block.shape[:3]
    for n in range(length):
        for v in range(variables):
            out[n, v] = block[n, jnp.where(plane == 0, 1, 0), v]


def tile_message_kernel(own, *rest, places):
    pieces, out = rest[:-1], rest[-1]
    length, variables = own.shape[:2]
    for n in range(length):
        for v in range(variables):
            out[0, n, v] = own[n, v]
            for p, piece in enumerate(pieces):
                out[p + 1, n, v] = piece[places[p], n, v]


def table_kernel(gain, counts, fold, fold_sine, tables):
    _, plane = place()
    face = jnp.where(plane == 0, 0, 1)
    rows, modes = fold.shape
    mode = lax.broadcasted_iota(jnp.int32, (modes, counts.shape[1]), 0)
    resolved = (mode < jnp.where(plane == 0, counts[:1], counts[1:])).astype(jnp.float32)
    outgoing = gain.shape[2]
    parts = []
    for part, table in enumerate((fold, fold_sine)):
        for o in range(outgoing):
            both = gain[face, part, o]
            parts += [table[...] * both[i : i + 1, :] for i in range(NI)]
    parts.append(fold[...])
    summed = jnp.dot(jnp.concatenate(parts, axis=0), resolved, precision=precise, preferred_element_type=jnp.float32)
    for k in range(len(parts)):
        tables[k] = summed[k * rows : (k + 1) * rows]


def rate_kernel(harmonics, state, *rest, inst_count):
    others = rest[: inst_count - 1]
    out_waves, in_waves, rates = rest[inst_count - 1 :]
    local_count, variables, cells, stations = state.shape
    total = local_count * inst_count
    width = out_waves.shape[1]
    half_width = width // 2
    lane = lax.broadcasted_iota(jnp.int32, (1, width), 1)
    lane = jnp.where(lane < half_width, lane, lane - half_width)
    present = jnp.zeros((1, width), jnp.float32)
    for k in range(harmonics.shape[0]):
        h = harmonics[k]
        residue = lax.rem(h, total)
        weight = h.astype(jnp.float32)
        present = present + jnp.where(lane == residue, weight, 0.0) - jnp.where(lane == total - residue, weight, 0.0)
    count = local_count * cells
    matrix = split_dot(out_waves[...] * present, in_waves[...])
    rows = lax.broadcasted_iota(jnp.int32, matrix.shape, 0)
    columns = lax.broadcasted_iota(jnp.int32, matrix.shape, 1)
    cell_of = (lambda x: x & (cells - 1)) if cells & (cells - 1) == 0 else (lambda x: lax.rem(x, cells))
    matrix = jnp.where(cell_of(rows) == cell_of(columns), matrix, 0.0)
    high, low = split_rows(matrix)
    left = jnp.concatenate([high, high, low], axis=1)
    flats = []
    for v in range(variables):
        sources = (state,) + tuple(others)
        flats.append(jnp.concatenate([source[:, v].reshape(count, stations) for source in sources], axis=0))
    b_high, b_low = split_rows(jnp.concatenate(flats, axis=1))
    right = jnp.concatenate([b_high, b_low, b_high], axis=0)
    rates[...] = jnp.dot(left, right, preferred_element_type=jnp.float32)


def jump_kernel(lefts, forward, backward, tables, own, *rest, tiles, planes, places, early):
    pieces, rest = rest[: planes - 1], rest[planes - 1 :]
    arrived, rest = rest[: tiles - 1], rest[tiles - 1 :]
    swapped, outs, gathered = rest[: len(early)], rest[len(early) : -1], rest[-1]
    tile, plane = place()
    count, variables, width, stations = own.shape
    blocks = [own] + [piece.at[at] for piece, at in zip(pieces, places)]
    for step in range(1, tiles):
        block = arrived[step - 1]
        if step in early:
            blocks += [block.at[:, jnp.where(plane == 0, 0, 1)], swapped[early.index(step)]]
        else:
            blocks += [block.at[p] for p in range(planes)]
    rows = tables.shape[1]
    cells = outs[0].shape[1]
    left = lambda u, v: lefts[u, v]
    position = tile * planes + plane if forward.shape[0] > planes else plane
    into, back_from = forward[position], backward[position]
    for t in range(count):
        for b, block in enumerate(blocks):
            for v in range(variables):
                gathered[t * variables + v, b * width : (b + 1) * width, :] = block[t, v]
        faces = jnp.concatenate([gathered[t * variables + v] for v in range(variables)], axis=1)
        hats = split_dot(into, faces)
        hats = [hats[:, v * stations : (v + 1) * stations] for v in range(variables)]
        wave = []
        for u in range(variables):
            acc = left(u, 0) * hats[0]
            for v in range(1, variables):
                acc = acc + left(u, v) * hats[v]
            wave.append((acc[:rows], acc[rows:]))
        jumps = []
        for i in range(NI):
            cos_part = -tables[12] * wave[i][0]
            sin_part = -tables[12] * wave[i][1]
            for o in range(variables - NI):
                out_cos, out_sin = wave[NI + o]
                real, imag = tables[o * NI + i], tables[6 + o * NI + i]
                cos_part = cos_part + real * out_cos - imag * out_sin
                sin_part = sin_part + imag * out_cos + real * out_sin
            jumps.append(jnp.concatenate([cos_part, sin_part], axis=0))
        back = split_dot(back_from, jnp.concatenate(jumps, axis=1))
        for k, out in enumerate(outs):
            for i in range(NI):
                out[t * NI + i] = back[k * cells : (k + 1) * cells, i * stations : (i + 1) * stations]


def block_start(tile, k, blocks, length):
    return partner(tile, k, blocks)[1] * length if blocks > 1 else 0


def axial_sign(plane):
    return jnp.where(plane == 0, -0.5, 0.5)


def flux_kernel(fluxes, state, inv_volume, *rest, planes, neighbours, groups):
    variables, cells, stations = state.shape[1:]
    pieces, rest = rest[: len(groups) * (planes - 1)], rest[len(groups) * (planes - 1) :]
    layers, rest = rest[: 2 * neighbours], rest[2 * neighbours :]
    half_count = layers[0].shape[0]
    lanes = lax.broadcasted_iota(jnp.int32, (cells, stations), 1)
    own, out = rest[:-1], rest[-1]
    volume = inv_volume[...]
    tile, plane = place()
    face_on = jnp.where(jnp.logical_or(plane == 0, plane == planes - 1), 1.0, 0.0)
    signs = [-axial_sign(plane)] if neighbours == 1 else [0.5, -0.5]
    axial = lambda v, w, sign: sign * fluxes[v, 0, w] - (DISSIPATION if v == w else 0.0)
    face_mat = [[face_on * axial(v, w, axial_sign(plane)) for w in range(variables)] for v in range(variables)]
    layer_mats = [[[axial(v, w, s) for w in range(variables)] for v in range(variables)] for s in signs]
    blocks = sum(len(g) for g in groups)
    length = pieces[0].shape[1]
    for k in range(blocks):
        start = block_start(tile, k, blocks, length)
        group = next(g for g, steps in enumerate(groups) if k in steps)
        at = groups[group].index(k)
        arrived = [pieces[p * len(groups) + group] for p in range(planes - 1)]

        def step(n, carry, k=k, start=start, arrived=arrived, at=at):
            t = start + n
            total, layer, along = [], [], []
            early = t < half_count
            sources = []
            for m in range(neighbours):
                low, high = layers[2 * m], layers[2 * m + 1]
                at_low, at_high = jnp.where(early, t, 0), jnp.where(early, 0, t - half_count)
                sources.append([jnp.where(early, low[at_low, w], high[at_high, w]) for w in range(variables)])
            for w in range(variables):
                s = state[t, w]
                right = jnp.where(lanes == stations - 1, 0.0, pltpu.roll(s, stations - 1, 1))
                left = jnp.where(lanes == 0, 0.0, pltpu.roll(s, 1, 1))
                along.append(0.5 * (right - left))
                total.append((6.0 * DISSIPATION) * s - DISSIPATION * (right + left))
                parts = [own[mirror(k, blocks)][n, w]] + [piece[at, n, w] for piece in arrived]
                ordered = [jnp.where(plane == 0, parts[j], parts[planes - 1 - j]) for j in range(planes)]
                layer.append(jnp.concatenate(ordered, axis=0))
            for v in range(variables):
                acc = total[v]
                for w in range(variables):
                    acc = acc + fluxes[v, 2, w] * along[w]
                    acc = acc + face_mat[v][w] * layer[w]
                    for mat, source in zip(layer_mats, sources):
                        acc = acc + mat[v][w] * source[w]
                out[t, v] = volume * acc
            return carry

        lax.fori_loop(0, length, step, 0, unroll=UNROLL)


def finish_kernel(fluxes, rights, inner, rates, inv_volume, state, *rest, planes, tiles, blocks):
    jumps, rest = rest[:blocks], rest[blocks:]
    halos, rest = rest[:2], rest[2:]
    own, (out, corrected, field, own_face, sems) = rest[:blocks], rest[blocks:]
    variables, width = own[0].shape[1:3]
    cells, stations = inner.shape[2:]
    row = lax.broadcasted_iota(jnp.int32, (cells, stations), 0)
    volume = inv_volume[...]
    tile, plane = place()
    face = jnp.where(plane == 0, 0, 1)
    face_on = jnp.where(jnp.logical_or(plane == 0, plane == planes - 1), 1.0, 0.0)
    right = [[rights[v, i] for i in range(NI)] for v in range(variables)]
    sign = axial_sign(plane)
    mixed = []
    for v in range(variables):
        mixed.append([])
        for i in range(NI):
            acc = -DISSIPATION * right[v][i]
            for w in range(variables):
                acc = acc + sign * fluxes[v, 0, w] * right[w][i]
            mixed[v].append(face_on * acc)
    length = own[0].shape[0]
    swapped = tile % 2 == 1 if tiles == 4 else tile < 0

    def halo_row(halo, index):
        return halo[lax.div(index, cells), pl.ds(lax.rem(index, cells), 1), :]

    copies = []
    for k, jump in enumerate(jumps):
        start = block_start(tile, k, blocks, length)
        faces = own[mirror(k, blocks)]

        def step(n, carry, jump=jump, start=start, faces=faces):
            t = start + n
            z = [jump[n * NI + i] for i in range(NI)]
            values = []
            for i in range(NI):
                value = z[i][:width]
                for j in range(1, planes):
                    value = jnp.where(plane == j, z[i][j * width : (j + 1) * width], value)
                values.append(value)
            half, total = [], []
            for w in range(variables):
                value = state[t, w]
                index = t * variables + w
                after, before = halo_row(halos[0], index), halo_row(halos[1], index)
                after, before = jnp.where(swapped, before, after), jnp.where(swapped, after, before)
                forward = jnp.where(row == cells - 1, after, pltpu.roll(value, cells - 1, 0))
                backward = jnp.where(row == 0, before, pltpu.roll(value, 1, 0))
                half.append(0.5 * (forward - backward))
                total.append(-DISSIPATION * (forward + backward))
            for v in range(variables):
                rate = rates[pl.ds(pl.multiple_of(t * cells, cells), cells), v * stations : (v + 1) * stations]
                acc = total[v] + (mixed[v][0] * z[0] + mixed[v][1] * z[1])
                for w in range(variables):
                    acc = acc + fluxes[v, 1, w] * half[w]
                field[t, v] = inner[t, v] + rate + volume * acc
                own_face[t, v] = faces[n, v] + right[v][0] * values[0] + right[v][1] * values[1]
            return carry

        lax.fori_loop(0, length, step, 0, unroll=UNROLL)
        part = pl.ds(start, length)
        copies.append(pltpu.make_async_copy(field.at[part], out.at[part], sems.at[2 * k]))
        copies.append(pltpu.make_async_copy(own_face.at[part], corrected.at[part, face], sems.at[2 * k + 1]))
        copies[-2].start()
        copies[-1].start()
    for copy in copies:
        copy.wait()


def back_kernel(*refs, shift, planes):
    jumps, out = refs[:-1], refs[-1]
    _, plane = place()
    at = jnp.where(plane == 0, shift, planes - 1 - shift)
    length, _, width, _ = out.shape
    length = length // len(jumps)
    for k, jump in enumerate(jumps):
        for n in range(length):
            for i in range(NI):
                z = jump[n * NI + i]
                value = z[:width]
                for j in range(1, planes):
                    value = jnp.where(at == j, z[j * width : (j + 1) * width], value)
                out[k * length + n, i] = value


def other_kernel(rights, *rest, planes, blocks, groups):
    backs, rest = rest[: planes - 1], rest[planes - 1 :]
    faces, (partial, corrected, values, sems) = rest[:-4], rest[-4:]
    variables = faces[0].shape[-3]
    tile, plane = place()
    right = [[rights[v, i] for i in range(NI)] for v in range(variables)]
    length = backs[0].shape[0] // blocks
    if planes == 2:
        copies = []
        for k in range(blocks):
            start = block_start(tile, k, blocks, length)
            group = next(g for g, steps in enumerate(groups) if mirror(k, blocks) in steps)
            at = groups[group].index(mirror(k, blocks))

            def step(n, carry, k=k, start=start, source=faces[group], at=at):
                z = [backs[0][k * length + n, i] for i in range(NI)]
                for v in range(variables):
                    values[0, start + n, v] = (
                        source[at, n, v] + right[v][0] * z[0] + right[v][1] * z[1]
                    )
                return carry

            lax.fori_loop(0, length, step, 0, unroll=UNROLL)
            part = pl.ds(start, length)
            other = jnp.where(plane == 0, 1, 0)
            copies.append(pltpu.make_async_copy(values.at[0, part], corrected.at[part, other], sems.at[k]))
            copies[-1].start()
        for copy in copies:
            copy.wait()
        return
    for p in range(2):

        @pl.when(plane != p * (planes - 1))
        def _():
            for k in range(blocks):
                start = block_start(tile, k, blocks, length)

                def step(n, carry, k=k, start=start):
                    z = []
                    for i in range(NI):
                        value = backs[0][k * length + n, i]
                        for s in range(2, planes):
                            at = s if p == 0 else planes - 1 - s
                            value = jnp.where(plane == at, backs[s - 1][k * length + n, i], value)
                        z.append(value)
                    for v in range(variables):
                        values[p, start + n, v] = (
                            faces[0][start + n, p, v] + right[v][0] * z[0] + right[v][1] * z[1]
                        )
                    return carry

                lax.fori_loop(0, length, step, 0, unroll=UNROLL)
            copy = pltpu.make_async_copy(values.at[p], corrected.at[:, p], sems.at[p])
            copy.start()
            copy.wait()


def face_groups(tiles):
    return FACE_GROUPS if tiles == 4 else [list(range(tiles))]


def mirror(k, blocks):
    return k if blocks in (1, 4) else (blocks - k) % blocks


ANY_SPEC = pl.BlockSpec(memory_space=pl.ANY)


def call(kernel, shapes, smem, arrays, scratch=(), hbm=(), final={}, aliases=None):
    arrays = [
        pltpu.with_memory_space_constraint(a, pltpu.HBM if i in hbm else pltpu.VMEM) for i, a in enumerate(arrays)
    ]
    return pl.pallas_call(
        kernel,
        out_shape=[s if i in final else pltpu.VMEM(s.shape, s.dtype) for i, s in enumerate(shapes)],
        in_specs=[SMEM_SPEC] * len(smem) + [ANY_SPEC if i in hbm else VMEM_SPEC for i in range(len(arrays))],
        out_specs=[final[i] if i in final else VMEM_SPEC for i in range(len(shapes))],
        scratch_shapes=scratch,
        input_output_aliases=aliases or {},
        compiler_params=pltpu.CompilerParams(vmem_limit_bytes=KERNEL_VMEM),
    )(*smem, *arrays)


def local(
    state,
    boundary,
    inv_volume,
    flux_matrix,
    left_vectors,
    right_vectors,
    gain,
    harmonic_index,
    mode_count,
):
    f32 = jnp.float32
    tiles, planes, insts = lax.axis_size("tile"), lax.axis_size("plane"), lax.axis_size("inst")
    count, variables, _, cells, stations = state.shape
    width = boundary.shape[3]
    period = width * tiles * planes
    modes = gain.shape[2]
    tile, plane = lax.axis_index("tile"), lax.axis_index("plane")
    time_parts = math.gcd(count, tiles)
    lane_parts = tiles // time_parts
    length, lanes = count // time_parts, stations // lane_parts
    own_face = jnp.where(plane == 0, 0, 1)
    field = state.reshape(count, variables, cells, stations)
    struct = lambda *shape: jax.ShapeDtypeStruct(shape, f32)
    by_kernel = lane_parts == 1
    blocks = tiles if by_kernel else 1

    def blocks_of(faces):
        split = faces.reshape(time_parts, length, variables, width, lane_parts, lanes)
        return lambda at: lax.dynamic_index_in_dim(
            lax.dynamic_index_in_dim(split, at // lane_parts, 0, keepdims=False), at % lane_parts, 3, keepdims=False
        )

    target = lambda step: partner(tile, step, tiles)[0]

    pieces, messages = [], []
    groups = face_groups(tiles) if by_kernel else [[0]]
    for shift in range(1, planes):
        pairs = [(shift, 0), (planes - 1 - shift, planes - 1)]
        if by_kernel:
            message = call(
                lambda *refs: face_message_kernel(*refs, groups=groups, shift=shift, tiles=tiles),
                [struct(len(steps), length, variables, width, stations) for steps in groups],
                (),
                (boundary,),
            )
        else:
            message = [lax.dynamic_index_in_dim(boundary, jnp.where(plane == shift, 0, 1), 1, keepdims=False)[None]]
        messages.append(message)
        pieces.append([lax.ppermute(part, "plane", pairs) for part in message])

    if by_kernel:
        own_blocks = call(
            lambda *refs: own_message_kernel(*refs, steps=range(tiles), tiles=tiles),
            [struct(length, variables, width, stations)] * tiles,
            (),
            (boundary,),
        )

        def take(step):
            group = next(g for g, steps in enumerate(groups) if step in steps)
            return [piece[group] for piece in pieces], [groups[group].index(step)] * len(pieces)

    else:
        take_own = blocks_of(lax.dynamic_index_in_dim(boundary, own_face, 1, keepdims=False))
        own_blocks = [take_own(target(step)) for step in range(tiles)]

        def take(step):
            return [blocks_of(piece[0][0])(target(step))[None] for piece in pieces], [0] * len(pieces)

    others = [lax.ppermute(field, "inst", [((i + s) % insts, i) for i in range(insts)]) for s in range(1, insts)]
    order = list(range(tiles - 1, 0, -1))
    home, home_places = take(0)
    arrived, swapped = {}, {}
    early = [EARLY] if tiles == 4 and planes == 2 and by_kernel else []
    for step in early:
        both = call(
            lambda *refs: early_message_kernel(*refs, step=step, tiles=tiles),
            [struct(length, *boundary.shape[1:])],
            (),
            (boundary,),
            [pltpu.SemaphoreType.DMA(())],
            hbm=(0,),
        )[0]
        arrived[step] = lax.ppermute(both, "tile", tile_pairs(step, tiles))
        part = call(swap_message_kernel, [struct(length, *boundary.shape[2:])], (), (arrived[step],))[0]
        swapped[step] = lax.ppermute(part, "plane", [(0, 1), (1, 0)])
    for step in order:
        if step in early:
            continue
        got, places = take(step)
        message = call(
            lambda *refs: tile_message_kernel(*refs, places=places),
            [struct(planes, *own_blocks[step].shape)],
            (),
            (own_blocks[step], *got),
        )[0]
        arrived[step] = lax.ppermute(message, "tile", tile_pairs(step, tiles))
    lines = -(-count * variables // cells)
    rows_out = call(
        lambda *refs: halo_message_kernel(*refs, tiles=tiles),
        [struct(lines, cells, stations)] * 2
        + [struct(part, *field.shape[1:]) for part in (count // 4, count - count // 4)],
        (),
        (field,),
    )
    rows_out, halves = rows_out[:2], rows_out[2:]
    if planes == 2:
        pairs = [[(0, 1), (1, 0)]]
    else:
        pairs = [[(i + 1, i) for i in range(planes - 1)], [(i, i + 1) for i in range(planes - 1)]]
    layers = [lax.ppermute(half, "plane", pair) for pair in pairs for half in halves]
    halos = [lax.ppermute(row, "tile", tile_pairs(step, tiles)) for row, step in zip(rows_out, (1, tiles - 1))]
    if tiles != 4:
        halos = halos[::-1]

    fluxes, lefts, rights = jnp.transpose(flux_matrix, (1, 0, 2)), left_vectors, right_vectors
    fold, fold_sine, rows, class_count = fold_tables(modes, period)
    total = count * insts
    out_waves, in_waves = rate_waves(count, total, cells)
    forward, backward = cell_layouts(tiles, planes, width, rows, class_count)
    face_gain = jnp.transpose(gain, (0, 1, 4, 3, 2))
    station_modes = mode_count
    if lane_parts > 1:
        station_modes = lax.dynamic_slice_in_dim(mode_count, (tile % lane_parts) * lanes, lanes, 1)
    volume = inv_volume.reshape(cells, stations)

    tables = call(
        table_kernel,
        [struct(13, rows, lanes)],
        (),
        (face_gain, station_modes, jnp.asarray(fold), jnp.asarray(fold_sine)),
    )[0]
    rates = call(
        lambda *refs: rate_kernel(*refs, inst_count=insts),
        [struct(count * cells, variables * stations)],
        (harmonic_index,),
        (field, *others, jnp.asarray(out_waves), jnp.asarray(in_waves)),
    )[0]
    jumps = call(
        lambda *refs: jump_kernel(*refs, tiles=tiles, planes=planes, places=home_places, early=early),
        [struct(length * NI, cells, lanes)] * tiles,
        (lefts,),
        (
            jnp.asarray(forward),
            jnp.asarray(backward),
            tables,
            own_blocks[0],
            *home,
            *[arrived[step] for step in range(1, tiles)],
            *[swapped[step] for step in early],
        ),
        [pltpu.VMEM((length * variables, period, lanes), f32)],
    )
    came = {0: jumps[0]}
    for step in order:
        came[step] = lax.ppermute(jumps[step], "tile", tile_pairs(step, tiles))
    jumps = [came[step] for step in range(tiles)]
    if not by_kernel:
        sources = np.array([[partner(i, s, tiles)[1] for s in range(tiles)] for i in range(tiles)])
        places = jnp.asarray(np.argsort(sources, axis=1))[tile]
        whole = jnp.take(jnp.stack(jumps), places, axis=0)
        whole = whole.reshape(time_parts, lane_parts, length, NI, cells, lanes)
        jumps = [jnp.transpose(whole, (0, 2, 3, 4, 1, 5)).reshape(count * NI, cells, stations)]
    if by_kernel:
        own_faces, other_faces = own_blocks, messages[0] if planes == 2 else [boundary]
    else:
        own_faces = [lax.dynamic_index_in_dim(boundary, own_face, 1, keepdims=False)]
        other_faces = messages[0] if planes == 2 else [boundary]
    backs = []
    for shift in range(1, planes):
        part = call(
            lambda *refs: back_kernel(*refs, shift=shift, planes=planes),
            [struct(count, NI, width, stations)],
            (),
            tuple(jumps),
        )[0]
        backs.append(lax.ppermute(part, "plane", [(0, shift), (planes - 1, planes - 1 - shift)]))

    inner = call(
        lambda *refs: flux_kernel(*refs, planes=planes, neighbours=len(layers) // 2, groups=groups),
        [struct(*field.shape)],
        (fluxes,),
        (field, volume, *[part for piece in pieces for part in piece], *layers, *own_faces),
    )[0]
    residual, partial = call(
        lambda *refs: finish_kernel(*refs, planes=planes, tiles=tiles, blocks=blocks),
        [struct(*field.shape), struct(*boundary.shape)],
        (fluxes, rights),
        (inner, rates, volume, field, *jumps, *halos, *own_faces),
        [
            pltpu.VMEM(field.shape, f32),
            pltpu.VMEM((count, variables, width, stations), f32),
            pltpu.SemaphoreType.DMA((2 * blocks,)),
        ],
        final={0: ANY_SPEC, 1: ANY_SPEC},
    )
    corrected = call(
        lambda *refs: other_kernel(*refs, planes=planes, blocks=blocks, groups=groups),
        [struct(*boundary.shape)],
        (rights,),
        (*backs, *other_faces, partial),
        [
            pltpu.VMEM((1 if planes == 2 else 2, count, variables, width, stations), f32),
            pltpu.SemaphoreType.DMA((max(blocks, 2),)),
        ],
        hbm=(len(backs) + len(other_faces),),
        final={0: ANY_SPEC},
        aliases={len(backs) + len(other_faces) + 1: 0},
    )[0]
    return (residual.reshape(state.shape), corrected)


def solution(mesh):
    return jax.shard_map(
        local,
        mesh=mesh,
        in_specs=(
            P("inst", "groups", "plane", "tile", None),
            P("inst", None, "groups", ("tile", "plane"), None),
            P(("groups", "plane"), "tile", None),
            P("groups", None, None),
            P("groups", None),
            P("groups", None),
            P("groups", None, None, None, None),
            P("groups"),
            P("groups", None),
        ),
        out_specs=(
            P("inst", "groups", "plane", "tile", None),
            P("inst", None, "groups", ("tile", "plane"), None),
        ),
        check_vma=False,
    )
```
